32 devices in a mesh: stream: 4 (over x, core), cross: 8 (over z, y).
Axes of the slice: x: 2, y: 2, z: 4, core: 2. Of those that a mesh axis runs over, the one named last changes fastest.
Arguments:
- state_now: float32 [7, 8, 64, 512], P(None, None, 'cross', 'stream'), as said below
- state_base: float32 [7, 8, 64, 512], P(None, None, 'cross', 'stream'), as said below
- inflow: float32 [7, 8, 64, 3], P(None, None, 'cross'), as said below
Outputs:
- state_next: float32 [7, 8, 64, 512], P(None, None, 'cross', 'stream')
Inputs may be any that keep to these rules, and one draw needn't show every extreme that they name: `state_now`: partial densities and volume fractions are positive, volume fractions below 1, and the pressure that each cell implies is positive. `state_base`: partial densities and volume fractions are positive, volume fractions below 1, and the pressure that each cell implies is positive. `inflow`: partial densities and volume fractions are positive, volume fractions below 1, and the pressure that each cell implies is positive.
All inputs are finite; a program needn't handle non-finite values.
Results may differ from the reference program's by a relative error of at most 0.0003.
Values sent between devices are 32-bit elements; how exact they have to be, the bound alone decides.
No kernel may reach another device: no remote copies, remote signals or barrier semaphores. Data moves between devices by JAX's collectives and lax.ppermute only.
A program may use at most 64 MiB of HBM per device.

```python
import jax
import jax.numpy as jnp
from jax import lax

CZ = 8
NX = 512
NY = 64


gas_gamma = 1.4


liquid_gamma = 4.4


liquid_stiff = 0.6


def field_cells(key, streamwise):
    subkeys = jax.random.split(key, 7)
    grid_shape = streamwise.shape
    lower_end = 0.5
    upper_end = 2.0
    volume = jax.random.uniform(subkeys[2], grid_shape, jnp.float32, 0.1, 0.9)

    def rough_field(subkey):
        return jnp.exp(jax.random.uniform(subkey, grid_shape, jnp.float32, jnp.log(lower_end), jnp.log(upper_end)))
    dens_gas = rough_field(subkeys[0])
    dens_liquid = 4.0 * rough_field(subkeys[1])
    stream_vel = (0.4 + 6.0 * streamwise) * jax.random.uniform(subkeys[3], grid_shape, jnp.float32, 0.8, 1.2)
    cross_vel = jax.random.uniform(subkeys[4], grid_shape, jnp.float32, -0.8, 0.8)
    span_vel = jax.random.uniform(subkeys[5], grid_shape, jnp.float32, -0.8, 0.8)
    pressure = rough_field(subkeys[6])
    partial_gas = volume * dens_gas
    partial_liquid = (1.0 - volume) * dens_liquid
    density = partial_gas + partial_liquid
    stiff_gamma = volume / (gas_gamma - 1.0) + (1.0 - volume) / (liquid_gamma - 1.0)
    stiff_term = (1.0 - volume) * liquid_gamma * liquid_stiff / (liquid_gamma - 1.0)
    energy = stiff_gamma * pressure + stiff_term + 0.5 * density * (stream_vel * stream_vel + cross_vel * cross_vel + span_vel * span_vel)
    return jnp.stack([partial_gas, partial_liquid, density * stream_vel, density * cross_vel, density * span_vel, energy, volume])


def grid_positions():
    positions = (jnp.arange(NX, dtype=jnp.float32) + 0.5) / NX
    return jnp.broadcast_to(positions, (CZ, NY, NX))


def draw_state_now(key, part):
    return field_cells(jax.random.fold_in(key, 11), grid_positions())


def draw_state_base(key, part):
    return field_cells(jax.random.fold_in(key, 23), grid_positions())


def draw_inflow(key, part):
    return field_cells(jax.random.fold_in(key, 37), jnp.ones((CZ, NY, 3), jnp.float32))


def setup_inputs(seed: int = 0) -> dict:
    key_list = jax.random.split(jax.random.key(seed), 4)
    return {
        "state_now": draw_state_now(jax.random.fold_in(key_list[3], 71), 0),
        "state_base": draw_state_base(jax.random.fold_in(key_list[3], 71), 0),
        "inflow": draw_inflow(jax.random.fold_in(key_list[3], 71), 0),
    }


gas_gamma = 1.4
liquid_gamma = 4.4
liquid_stiff = 0.6
courant = 0.3
weno_epsilon = 1e-06

def mixture(volume):
    stiff_gamma = volume / (gas_gamma - 1.0) + (1.0 - volume) / (liquid_gamma - 1.0)
    stiff_term = (1.0 - volume) * liquid_gamma * liquid_stiff / (liquid_gamma - 1.0)
    return (stiff_gamma, stiff_term)

def primitive(conserved):
    density = conserved[0] + conserved[1]
    vel_one = conserved[2] / density
    vel_two = conserved[3] / density
    vel_three = conserved[4] / density
    kinetic = 0.5 * (conserved[2] * vel_one + conserved[3] * vel_two + conserved[4] * vel_three)
    stiff_gamma, stiff_term = mixture(conserved[6])
    pressure = (conserved[5] - kinetic - stiff_term) / stiff_gamma
    return jnp.stack([conserved[0], conserved[1], vel_one, vel_two, vel_three, pressure, conserved[6]])

def sound(primitives):
    density = primitives[0] + primitives[1]
    stiff_gamma, stiff_term = mixture(primitives[6])
    return jnp.sqrt(((stiff_gamma + 1.0) * primitives[5] + stiff_term) / (stiff_gamma * density))

def max_speed(conserved):
    primitives = primitive(conserved)
    fastest = jnp.maximum(jnp.maximum(jnp.abs(primitives[2]), jnp.abs(primitives[3])), jnp.abs(primitives[4]))
    return jnp.max(fastest + sound(primitives))

def weno_face(far_left, near_left, centre, near_right, far_right):
    first_low = far_left - 2.0 * near_left + centre
    second_low = far_left - 4.0 * near_left + 3.0 * centre
    first_mid = near_left - 2.0 * centre + near_right
    second_mid = near_left - near_right
    first_high = centre - 2.0 * near_right + far_right
    second_high = 3.0 * centre - 4.0 * near_right + far_right
    smooth_low = weno_epsilon + 13.0 / 12.0 * first_low * first_low + 0.25 * second_low * second_low
    smooth_mid = weno_epsilon + 13.0 / 12.0 * first_mid * first_mid + 0.25 * second_mid * second_mid
    smooth_high = weno_epsilon + 13.0 / 12.0 * first_high * first_high + 0.25 * second_high * second_high
    weight_low = 0.1 / (smooth_low * smooth_low)
    weight_mid = 0.6 / (smooth_mid * smooth_mid)
    weight_high = 0.3 / (smooth_high * smooth_high)
    guess_low = (2.0 * far_left - 7.0 * near_left + 11.0 * centre) / 6.0
    guess_mid = (-near_left + 5.0 * centre + 2.0 * near_right) / 6.0
    guess_high = (2.0 * centre + 5.0 * near_right - far_right) / 6.0
    return (weight_low * guess_low + weight_mid * guess_mid + weight_high * guess_high) / (weight_low + weight_mid + weight_high)

def clamp_face(state, lower_cell, upper_cell):
    smaller = jnp.minimum(lower_cell, upper_cell)
    larger = jnp.maximum(lower_cell, upper_cell)
    limited = []
    for component in range(7):
        face_value = state[component]
        if component in (0, 1, 5):
            face_value = jnp.maximum(face_value, 0.5 * smaller[component])
        elif component == 6:
            face_value = jnp.clip(face_value, 0.5 * smaller[6], 1.0 - 0.5 * (1.0 - larger[6]))
        limited.append(face_value)
    return jnp.stack(limited)

def side_terms(primitives, normal):
    density = primitives[0] + primitives[1]
    stiff_gamma, stiff_term = mixture(primitives[6])
    velocity = [primitives[2], primitives[3], primitives[4]]
    energy = stiff_gamma * primitives[5] + stiff_term + 0.5 * density * (velocity[0] * velocity[0] + velocity[1] * velocity[1] + velocity[2] * velocity[2])
    normal_vel = velocity[normal]
    amounts = jnp.stack([primitives[0], primitives[1], density * velocity[0], density * velocity[1], density * velocity[2], energy, primitives[6]])
    momentum = []
    for component in range(3):
        moved = density * velocity[component] * normal_vel
        if component == normal:
            moved = moved + primitives[5]
        momentum.append(moved)
    transport = jnp.stack([primitives[0] * normal_vel, primitives[1] * normal_vel, momentum[0], momentum[1], momentum[2], (energy + primitives[5]) * normal_vel, primitives[6] * normal_vel])
    signal = jnp.abs(normal_vel) + sound(primitives)
    return (amounts, transport, normal_vel, signal)

def face_flux(left_state, right_state, normal):
    amount_left, transport_left, normal_left, signal_left = side_terms(left_state, normal)
    amount_right, transport_right, normal_right, signal_right = side_terms(right_state, normal)
    fastest = jnp.maximum(signal_left, signal_right)
    face_fluxes = 0.5 * (transport_left + transport_right) - 0.5 * fastest * (amount_right - amount_left)
    return (face_fluxes, 0.5 * (normal_left + normal_right))

def direction_sweep(padded, dimension, normal):
    primitives = primitive(padded)
    length = padded.shape[dimension] - 6
    pieces = [lax.slice_in_dim(primitives, offset, offset + length + 1, axis=dimension) for offset in range(6)]
    left_state = clamp_face(weno_face(pieces[0], pieces[1], pieces[2], pieces[3], pieces[4]), pieces[2], pieces[3])
    right_state = clamp_face(weno_face(pieces[5], pieces[4], pieces[3], pieces[2], pieces[1]), pieces[2], pieces[3])
    face_fluxes, face_motion = face_flux(left_state, right_state, normal)
    change = lax.slice_in_dim(face_fluxes, 1, length + 1, axis=dimension) - lax.slice_in_dim(face_fluxes, 0, length, axis=dimension)
    spread = lax.slice_in_dim(face_motion, 1, length + 1, axis=dimension - 1) - lax.slice_in_dim(face_motion, 0, length, axis=dimension - 1)
    return (change, spread)

def tendency(stream_cells, cross_cells, span_cells, centre_cells):
    change_stream, spread_stream = direction_sweep(stream_cells, 3, 0)
    change_cross, spread_cross = direction_sweep(cross_cells, 2, 1)
    change_span, spread_span = direction_sweep(span_cells, 1, 2)
    total = -(change_stream + change_cross + change_span)
    source = centre_cells[6] * (spread_stream + spread_cross + spread_span)
    return jnp.concatenate([total[:6], (total[6] + source)[None]], axis=0)

def reference(state_now, state_base, inflow):

    def plane_max(plane_index):
        return max_speed(lax.dynamic_slice_in_dim(state_base, plane_index, 1, 1))
    fastest = jnp.max(lax.map(plane_max, jnp.arange(CZ, dtype=jnp.int32)))
    time_step = courant / fastest
    last_cells = jnp.repeat(state_now[:, :, :, -1:], 3, axis=3)
    stream_padded = jnp.concatenate([inflow, state_now, last_cells], axis=3)
    cross_padded = jnp.concatenate([stream_padded[:, :, -3:], stream_padded, stream_padded[:, :, :3]], axis=2)
    padded = jnp.concatenate([cross_padded[:, -3:], cross_padded, cross_padded[:, :3]], axis=1)

    def one_plane(plane_index):
        span_cells = lax.dynamic_slice_in_dim(padded, plane_index, 7, 1)[:, :, 3:-3, 3:-3]
        middle = lax.dynamic_slice_in_dim(padded, plane_index + 3, 1, 1)
        cross_cells = middle[:, :, :, 3:-3]
        stream_cells = middle[:, :, 3:-3, :]
        centre_cells = middle[:, :, 3:-3, 3:-3]
        changes = tendency(stream_cells, cross_cells, span_cells, centre_cells)
        base_plane = lax.dynamic_slice_in_dim(state_base, plane_index, 1, 1)
        updated = base_plane / 3.0 + 2.0 / 3.0 * (centre_cells + time_step * changes)
        return updated[:, 0]
    planes = lax.map(one_plane, jnp.arange(CZ, dtype=jnp.int32))
    return jnp.transpose(planes, (1, 0, 2, 3))
```

```python
import functools

import jax
import jax.numpy as jnp
from jax import lax
from jax.experimental import pallas as pl
from jax.experimental.pallas import tpu as pltpu
from jax.sharding import PartitionSpec as P

gas_gamma = 1.4
liquid_gamma = 4.4
liquid_stiff = 0.6
courant = 0.3
weno_epsilon = 1e-06
ghost = 3
fields = 7


def reciprocal(value):
    guess = pl.reciprocal(value, approx=True)
    return guess * (2.0 - value * guess)


def mixture(volume):
    rest = 1.0 - volume
    stiff_gamma = volume * (1.0 / (gas_gamma - 1.0)) + rest * (1.0 / (liquid_gamma - 1.0))
    stiff_term = rest * (liquid_gamma * liquid_stiff / (liquid_gamma - 1.0))
    return stiff_gamma, stiff_term


def primitive(u):
    inverse = reciprocal(u[0] + u[1])
    v = [u[2] * inverse, u[3] * inverse, u[4] * inverse]
    kinetic = 0.5 * (u[2] * v[0] + u[3] * v[1] + u[4] * v[2])
    stiff_gamma, stiff_term = mixture(u[6])
    pressure = (u[5] - kinetic - stiff_term) * reciprocal(stiff_gamma)
    return [u[0], u[1], v[0], v[1], v[2], pressure, u[6]]


def sound(w, density, stiff_gamma, stiff_term):
    top = (stiff_gamma + 1.0) * w[5] + stiff_term
    return jnp.sqrt(top * reciprocal(stiff_gamma * density))


def weno_cell(a, b, c, d, h):
    low, mid, high = b - a, c - b, d - c
    e_low, e_mid, e_high = 3.0 * b - a, b + c, d - 3.0 * c

    def weight(bend, slope):
        smooth = weno_epsilon + (13.0 / 12.0) * (bend * bend) + 0.25 * (slope * slope)
        r = reciprocal(jnp.minimum(smooth, 1e38))
        return r * r

    w_low, w_mid, w_high = weight(low, e_low), 6.0 * weight(mid, e_mid), weight(high, e_high)
    low3, high3 = 3.0 * w_low, 3.0 * w_high
    total_up = (w_low + high3) + w_mid
    total_down = (low3 + w_high) + w_mid
    up = w_low * (5.0 * b - 2.0 * a) + w_mid * (b + 2.0 * c) + high3 * (4.0 * c - d)
    down = w_high * (5.0 * c - 2.0 * d) + w_mid * (c + 2.0 * b) + low3 * (4.0 * b - a)
    up = h + up * (reciprocal(total_up) * (1.0 / 6.0))
    down = h - down * (reciprocal(total_down) * (1.0 / 6.0))
    return up, down


def limit(component, value, first, second):
    if component in (0, 1, 5):
        return jnp.maximum(value, 0.5 * jnp.minimum(first, second))
    if component == 6:
        smaller = 0.5 * jnp.minimum(first, second)
        larger = 1.0 - 0.5 * (1.0 - jnp.maximum(first, second))
        return jnp.minimum(jnp.maximum(value, smaller), larger)
    return value


def cell_faces(component, a, b, c, d, h):
    up, down = weno_cell(a, b, c, d, h)
    return limit(component, up, h, h + c), limit(component, down, h - b, h)


def side_terms(w, normal):
    density = w[0] + w[1]
    stiff_gamma, stiff_term = mixture(w[6])
    v = w[2:5]
    mom = [density * x for x in v]
    energy = stiff_gamma * w[5] + stiff_term + 0.5 * (mom[0] * v[0] + mom[1] * v[1] + mom[2] * v[2])
    vn = v[normal]
    amounts = [w[0], w[1], mom[0], mom[1], mom[2], energy, w[6]]
    moved = [x * vn for x in amounts]
    moved[2 + normal] = moved[2 + normal] + w[5]
    moved[5] = moved[5] + w[5] * vn
    return amounts, moved, vn, jnp.abs(vn) + sound(w, density, stiff_gamma, stiff_term)


def face_flux(left, right, normal):
    ul, fl, vl, sl = side_terms(left, normal)
    ur, fr, vr, sr = side_terms(right, normal)
    half = 0.5 * jnp.maximum(sl, sr)
    flux = [0.5 * (fl[i] + fr[i]) - half * (ur[i] - ul[i]) for i in range(fields)]
    return flux + [0.5 * (vl + vr)]


def lane_of(shape):
    return lax.broadcasted_iota(jnp.int32, shape, 1)


def pack_kernel(now_ref, base_ref, inflow_ref, w_ref, up_ref, down_ref, edge_ref, in_ref):
    nz, ny, nx = now_ref.shape[1:]
    seg = nx // ny
    lane = lane_of((nz, nx))

    edge_ref[...] = jnp.zeros(edge_ref.shape, jnp.float32)
    fastest = None
    for y in range(ny):
        w = primitive([now_ref[c, :, y, :] for c in range(fields)])
        first = (lane >= y * seg) & (lane < y * seg + 5)
        mine = (lane >= y * seg) & (lane < (y + 1) * seg)
        for c in range(fields):
            w_ref[y, c] = w[c]
            if y >= ny - ghost:
                up_ref[(y - ny + ghost) * fields + c] = w[c]
            if y < ghost:
                down_ref[y * fields + c] = w[c]
            low = pltpu.roll(w[c], (y * seg + 3) % nx, 1)
            high = pltpu.roll(w[c], (y * seg + 10) % nx, 1)
            edge_ref[c] = jnp.where(mine, jnp.where(first, low, high), edge_ref[c])
        b = primitive([base_ref[c, :, y, :] for c in range(fields)])
        stiff_gamma, stiff_term = mixture(b[6])
        speed = jnp.maximum(jnp.maximum(jnp.abs(b[2]), jnp.abs(b[3])), jnp.abs(b[4]))
        speed = speed + sound(b, b[0] + b[1], stiff_gamma, stiff_term)
        fastest = speed if fastest is None else jnp.maximum(fastest, speed)
    up_ref[ghost * fields] = fastest
    down_ref[ghost * fields] = fastest
    edge_ref[fields] = fastest
    inner = primitive([inflow_ref[c] for c in range(fields)])
    for c in range(fields):
        in_ref[c] = inner[c]


def span_kernel(w_ref, rate_ref):
    ny = w_ref.shape[0]
    nz = w_ref.shape[2]

    def plane(y, _):
        left, right = [], []
        for k in range(fields):
            h = w_ref[y, k]
            c = pltpu.roll(h, nz - 1, 0) - h
            b = pltpu.roll(c, 1, 0)
            a = pltpu.roll(c, 2, 0)
            d = pltpu.roll(c, nz - 1, 0)
            up, down = cell_faces(k, a, b, c, d, h)
            left.append(pltpu.roll(up, 1, 0))
            right.append(down)
        flux = face_flux(left, right, 2)
        diff = [pltpu.roll(f, nz - 1, 0) - f for f in flux]
        for k in range(fields):
            rate_ref[y, k] = -diff[k] if k < 6 else w_ref[y, 6] * diff[7] - diff[6]
        return 0

    lax.fori_loop(0, ny, plane, 0)


def main_kernel(
    place_ref, w_ref, rate_ref, low_ref, high_ref, edge_ref, left_ref, right_ref, in_ref,
    speed_ref, now_ref, base_ref, out_ref,
    tall, ring, sides, seam, flux_ref, keep, acc,
):
    ny, _, nz, nx = w_ref.shape
    seg = nx // ny
    lane = lane_of((nz, nx))
    part = lane % seg
    is_first = place_ref[0] == 1
    is_last = place_ref[1] == 1

    for y in range(ghost):
        for c in range(fields):
            tall[y, c] = low_ref[y * fields + c]
            tall[ghost + ny + y, c] = high_ref[y * fields + c]

    def copy(y, _):
        tall[y + ghost] = w_ref[y]
        return 0

    lax.fori_loop(0, ny, copy, 0)

    def cross(i, _):
        left = [keep[k] for k in range(fields)]
        right = []
        for k in range(fields):
            f, g, h, kk, l = [tall[i + o, k] for o in range(5)]
            up, down = cell_faces(k, g - f, h - g, kk - h, l - kk, h)
            keep[k] = up
            right.append(down)

        @pl.when(i > 0)
        def _():
            flux = face_flux(left, right, 1)

            @pl.when(i > 1)
            def _():
                y = i - 2
                diff = [flux[k] - keep[fields + k] for k in range(fields + 1)]
                for k in range(6):
                    acc[y, k] = rate_ref[y, k] - diff[k]
                acc[y, 6] = rate_ref[y, 6] - diff[6] + w_ref[y, 6] * diff[7]

            for k in range(fields + 1):
                keep[fields + k] = flux[k]

        return 0

    lax.fori_loop(0, ny + 2, cross, 0)

    for k in range(fields):
        e = edge_ref[k]
        last = jnp.where(
            part == 10, pltpu.roll(e, 1, 1), jnp.where(part == 11, pltpu.roll(e, 2, 1), pltpu.roll(e, 3, 1))
        )
        lower = jnp.where(is_first, in_ref[k], left_ref[k])
        upper = jnp.where(is_last, last, right_ref[k])
        e = jnp.where(part < 3, lower, jnp.where((part >= 10) & (part < 13), upper, e))
        c = pltpu.roll(e, nx - 1, 1) - e
        ring[k] = c
        up, down = cell_faces(
            k, pltpu.roll(c, 2, 1), pltpu.roll(c, 1, 1), c, pltpu.roll(c, nx - 1, 1), e
        )
        sides[k] = up
        sides[fields + k] = down

    def stream(y, _):
        base = y * seg
        left, right = [], []
        at_seam = lane == base + 10
        for k in range(fields):
            h = w_ref[y, k]
            de = ring[k]
            tail = pltpu.roll(de, nx - 11 - base, 1)
            head = pltpu.roll(de, nx - 1 - base, 1)
            c = jnp.where(lane == nx - 1, pltpu.roll(tail, 1, 1), pltpu.roll(h, nx - 1, 1) - h)
            d = jnp.where(lane == nx - 1, tail, pltpu.roll(c, nx - 1, 1))
            a = jnp.where(lane < 2, head, pltpu.roll(c, 2, 1))
            b = jnp.where(lane < 1, pltpu.roll(head, nx - 1, 1), pltpu.roll(c, 1, 1))
            up, down = cell_faces(k, a, b, c, d, h)
            seam[k] = jnp.where(at_seam, pltpu.roll(up, base + 11, 1), seam[k])
            edge_up = pltpu.roll(sides[k], nx - base - 2, 1)
            left.append(jnp.where(lane < 1, edge_up, pltpu.roll(up, 1, 1)))
            right.append(down)
        flux = face_flux(left, right, 0)
        for k in range(fields + 1):
            flux_ref[y, k] = flux[k]
        return 0

    lax.fori_loop(0, ny, stream, 0)
    outer = face_flux(
        [seam[k] for k in range(fields)], [sides[fields + k] for k in range(fields)], 0
    )
    for k in range(fields + 1):
        keep[k] = outer[k]

    fastest = jnp.max(speed_ref[...])
    step = courant / jnp.full((nz, nx), fastest, jnp.float32)

    for y in range(ny):
        diff = []
        for k in range(fields + 1):
            f = flux_ref[y, k]
            end = pltpu.roll(keep[k], (2 * nx - 1 - 10 - y * seg) % nx, 1)
            diff.append(jnp.where(lane == nx - 1, end, pltpu.roll(f, nx - 1, 1)) - f)
        for k in range(fields):
            rate = acc[y, k] - diff[k]
            if k == 6:
                rate = rate + w_ref[y, 6] * diff[7]
            out_ref[k, :, y, :] = base_ref[k, :, y, :] * (1.0 / 3.0) + (2.0 / 3.0) * (
                now_ref[k, :, y, :] + step * rate
            )


def tile(count, nz, nx):
    return jax.ShapeDtypeStruct((count, nz, nx), jnp.float32)


def ring_pairs(size, shift):
    return [(i, (i + shift) % size) for i in range(size)]


def shards(state_now, state_base, inflow):
    _, nz, ny, nx = state_now.shape
    seg = nx // ny
    width = ghost * fields + 1
    packed = jnp.pad(inflow, ((0, 0), (0, 0), (0, 0), (0, seg - ghost))).reshape(fields, nz, nx)
    wide = jax.ShapeDtypeStruct((ny, fields, nz, nx), jnp.float32)
    w, up, down, edge, inner = pl.pallas_call(
        pack_kernel,
        out_shape=(
            wide,
            tile(width, nz, nx),
            tile(width, nz, nx),
            tile(fields + 1, nz, nx),
            tile(fields, nz, nx),
        ),
        name="pack",
    )(state_now, state_base, packed)

    streams, crosses = lax.axis_size("stream"), lax.axis_size("cross")
    low = lax.ppermute(up, "cross", ring_pairs(crosses, 1))
    high = lax.ppermute(down, "cross", ring_pairs(crosses, -1))
    left = lax.ppermute(edge, "stream", ring_pairs(streams, 1))
    right = lax.ppermute(edge, "stream", ring_pairs(streams, -1))

    rate = pl.pallas_call(span_kernel, out_shape=wide, name="span")(w)

    speed = jnp.maximum(jnp.maximum(low[-1], high[-1]), edge[-1])
    reach = 3
    while reach < crosses:
        ahead = lax.ppermute(speed, "cross", ring_pairs(crosses, reach))
        behind = lax.ppermute(speed, "cross", ring_pairs(crosses, -reach))
        speed = jnp.maximum(speed, jnp.maximum(ahead, behind))
        reach *= 3
    if streams & (streams - 1) == 0:
        hop = 1
        while hop < streams:
            pairs = [(i, i ^ hop) for i in range(streams)]
            speed = jnp.maximum(speed, lax.ppermute(speed, "stream", pairs))
            hop *= 2
    else:
        speed = functools.reduce(
            jnp.maximum,
            [lax.ppermute(speed, "stream", ring_pairs(streams, s)) for s in range(1, streams)],
            speed,
        )

    position = lax.axis_index("stream")
    place = jnp.stack([position == 0, position == streams - 1]).astype(jnp.int32)
    vmem = pl.BlockSpec(memory_space=pltpu.VMEM)
    return pl.pallas_call(
        main_kernel,
        out_shape=jax.ShapeDtypeStruct(state_now.shape, jnp.float32),
        in_specs=[pl.BlockSpec(memory_space=pltpu.SMEM)] + [vmem] * 11,
        scratch_shapes=[
            pltpu.VMEM((ny + 2 * ghost, fields, nz, nx), jnp.float32),
            pltpu.VMEM((fields, nz, nx), jnp.float32),
            pltpu.VMEM((2 * fields, nz, nx), jnp.float32),
            pltpu.VMEM((fields, nz, nx), jnp.float32),
            pltpu.VMEM((ny, fields + 1, nz, nx), jnp.float32),
            pltpu.VMEM((2 * fields + 1, nz, nx), jnp.float32),
            pltpu.VMEM((ny, fields, nz, nx), jnp.float32),
        ],
        name="sweep",
    )(place, w, rate, low, high, edge, left, right, inner, speed, state_now, state_base)


def solution(mesh):
    return jax.shard_map(
        shards,
        mesh=mesh,
        in_specs=(
            P(None, None, "cross", "stream"),
            P(None, None, "cross", "stream"),
            P(None, None, "cross", None),
        ),
        out_specs=P(None, None, "cross", "stream"),
        check_vma=False,
    )
```

```python
import jax
import jax.numpy as jnp
from jax import lax
from jax.experimental import pallas as pl
from jax.experimental.pallas import tpu as pltpu
from jax.sharding import PartitionSpec as P

gas_gamma = 1.4
liquid_gamma = 4.4
liquid_stiff = 0.6
courant = 0.3
weno_epsilon = 1e-06
ghost = 3
fields = 7


def reciprocal(value):
    guess = pl.reciprocal(value, approx=True)
    return guess * (2.0 - value * guess)


def mixture(volume):
    rest = 1.0 - volume
    stiff_gamma = volume * (1.0 / (gas_gamma - 1.0)) + rest * (1.0 / (liquid_gamma - 1.0))
    stiff_term = rest * (liquid_gamma * liquid_stiff / (liquid_gamma - 1.0))
    return stiff_gamma, stiff_term


def primitive(u):
    inverse = reciprocal(u[0] + u[1])
    v = [u[2] * inverse, u[3] * inverse, u[4] * inverse]
    kinetic = 0.5 * (u[2] * v[0] + u[3] * v[1] + u[4] * v[2])
    stiff_gamma, stiff_term = mixture(u[6])
    pressure = (u[5] - kinetic - stiff_term) * reciprocal(stiff_gamma)
    return [u[0], u[1], v[0], v[1], v[2], pressure, u[6]]


def sound(w, density, stiff_gamma, stiff_term):
    top = (stiff_gamma + 1.0) * w[5] + stiff_term
    return jnp.sqrt(top * reciprocal(stiff_gamma * density))


def weno_cell(a, b, c, d, h):
    low, mid, high = b - a, c - b, d - c
    e_low, e_mid, e_high = 3.0 * b - a, b + c, d - 3.0 * c

    def weight(bend, slope):
        smooth = weno_epsilon + (13.0 / 12.0) * (bend * bend) + 0.25 * (slope * slope)
        r = reciprocal(jnp.minimum(smooth, 1e38))
        return r * r

    w_low, w_mid, w_high = weight(low, e_low), 6.0 * weight(mid, e_mid), weight(high, e_high)
    low3, high3 = 3.0 * w_low, 3.0 * w_high
    total_up = (w_low + high3) + w_mid
    total_down = (low3 + w_high) + w_mid
    up = w_low * (5.0 * b - 2.0 * a) + w_mid * (b + 2.0 * c) + high3 * (4.0 * c - d)
    down = w_high * (5.0 * c - 2.0 * d) + w_mid * (c + 2.0 * b) + low3 * (4.0 * b - a)
    up = h + up * (reciprocal(total_up) * (1.0 / 6.0))
    down = h - down * (reciprocal(total_down) * (1.0 / 6.0))
    return up, down


def limit(component, value, first, second):
    if component in (0, 1, 5):
        return jnp.maximum(value, 0.5 * jnp.minimum(first, second))
    if component == 6:
        smaller = 0.5 * jnp.minimum(first, second)
        larger = 1.0 - 0.5 * (1.0 - jnp.maximum(first, second))
        return jnp.minimum(jnp.maximum(value, smaller), larger)
    return value


def cell_faces(component, a, b, c, d, h):
    up, down = weno_cell(a, b, c, d, h)
    return limit(component, up, h, h + c), limit(component, down, h - b, h)


def side_terms(w, normal):
    density = w[0] + w[1]
    stiff_gamma, stiff_term = mixture(w[6])
    v = w[2:5]
    mom = [density * x for x in v]
    energy = stiff_gamma * w[5] + stiff_term + 0.5 * (mom[0] * v[0] + mom[1] * v[1] + mom[2] * v[2])
    vn = v[normal]
    amounts = [w[0], w[1], mom[0], mom[1], mom[2], energy, w[6]]
    moved = [x * vn for x in amounts]
    moved[2 + normal] = moved[2 + normal] + w[5]
    moved[5] = moved[5] + w[5] * vn
    return amounts, moved, vn, jnp.abs(vn) + sound(w, density, stiff_gamma, stiff_term)


def face_flux(left, right, normal):
    ul, fl, vl, sl = side_terms(left, normal)
    ur, fr, vr, sr = side_terms(right, normal)
    half = 0.5 * jnp.maximum(sl, sr)
    flux = [0.5 * (fl[i] + fr[i]) - half * (ur[i] - ul[i]) for i in range(fields)]
    return flux + [0.5 * (vl + vr)]


def lane_of(shape):
    return lax.broadcasted_iota(jnp.int32, shape, 1)


def pack_kernel(now_ref, base_ref, w_ref, up_ref, down_ref, edge_ref):
    nz, ny, nx = now_ref.shape[1:]
    seg = nx // ny
    lane = lane_of((nz, nx))

    edge_ref[...] = jnp.zeros(edge_ref.shape, jnp.float32)
    fastest = None
    for y in range(ny):
        w = primitive([now_ref[c, :, y, :] for c in range(fields)])
        first = (lane >= y * seg) & (lane < y * seg + 5)
        mine = (lane >= y * seg) & (lane < (y + 1) * seg)
        for c in range(fields):
            w_ref[y, c] = w[c]
            if y >= ny - ghost:
                up_ref[(y - ny + ghost) * fields + c] = w[c]
            if y < ghost:
                down_ref[y * fields + c] = w[c]
            low = pltpu.roll(w[c], (y * seg + 3) % nx, 1)
            high = pltpu.roll(w[c], (y * seg + 10) % nx, 1)
            edge_ref[c] = jnp.where(mine, jnp.where(first, low, high), edge_ref[c])
        b = primitive([base_ref[c, :, y, :] for c in range(fields)])
        stiff_gamma, stiff_term = mixture(b[6])
        speed = jnp.maximum(jnp.maximum(jnp.abs(b[2]), jnp.abs(b[3])), jnp.abs(b[4]))
        speed = speed + sound(b, b[0] + b[1], stiff_gamma, stiff_term)
        fastest = speed if fastest is None else jnp.maximum(fastest, speed)
    up_ref[ghost * fields] = fastest
    down_ref[ghost * fields] = fastest
    edge_ref[fields] = fastest


def span_kernel(w_ref, inflow_ref, rate_ref, in_ref):
    ny, _, nz, nx = w_ref.shape
    seg = nx // ny

    def plane(y, _):
        left, right = [], []
        for k in range(fields):
            h = w_ref[y, k]
            c = pltpu.roll(h, nz - 1, 0) - h
            b = pltpu.roll(c, 1, 0)
            a = pltpu.roll(c, 2, 0)
            d = pltpu.roll(c, nz - 1, 0)
            up, down = cell_faces(k, a, b, c, d, h)
            left.append(pltpu.roll(up, 1, 0))
            right.append(down)
        flux = face_flux(left, right, 2)
        diff = [pltpu.roll(f, nz - 1, 0) - f for f in flux]
        for k in range(fields):
            rate_ref[y, k] = -diff[k] if k < 6 else w_ref[y, 6] * diff[7] - diff[6]
        return 0

    lax.fori_loop(0, ny, plane, 0)

    lane = lane_of((nz, nx))
    layers = []
    for c in range(fields):
        packed = jnp.ones((nz, nx), jnp.float32)
        for g in range(ghost):
            layer = jnp.concatenate(
                [inflow_ref[c, g], jnp.zeros((nz, nx - ny), jnp.float32)], axis=1
            )
            for y in range(ny):
                shift = (y * seg + g - y) % nx
                moved = layer if shift == 0 else pltpu.roll(layer, shift, 1)
                packed = jnp.where(lane == y * seg + g, moved, packed)
        layers.append(packed)
    layers = primitive(layers)
    for c in range(fields):
        in_ref[c] = layers[c]


def cross_kernel(w_ref, rate_ref, low_ref, high_ref, acc, tall, keep):
    ny = w_ref.shape[0]

    for y in range(ghost):
        for c in range(fields):
            tall[y, c] = low_ref[y * fields + c]
            tall[ghost + ny + y, c] = high_ref[y * fields + c]

    def copy(y, _):
        tall[y + ghost] = w_ref[y]
        return 0

    lax.fori_loop(0, ny, copy, 0)

    def cross(i, _):
        left = [keep[k] for k in range(fields)]
        right = []
        for k in range(fields):
            f, g, h, kk, l = [tall[i + o, k] for o in range(5)]
            up, down = cell_faces(k, g - f, h - g, kk - h, l - kk, h)
            keep[k] = up
            right.append(down)

        @pl.when(i > 0)
        def _():
            flux = face_flux(left, right, 1)

            @pl.when(i > 1)
            def _():
                y = i - 2
                diff = [flux[k] - keep[fields + k] for k in range(fields + 1)]
                for k in range(6):
                    acc[y, k] = rate_ref[y, k] - diff[k]
                acc[y, 6] = rate_ref[y, 6] - diff[6] + w_ref[y, 6] * diff[7]

            for k in range(fields + 1):
                keep[fields + k] = flux[k]

        return 0

    lax.fori_loop(0, ny + 2, cross, 0)


def stream_kernel(
    place_ref, w_ref, edge_ref, left_ref, right_ref, in_ref, acc_ref, rate_ref,
    ring, sides, seam, flux_ref, keep,
):
    ny, _, nz, nx = w_ref.shape
    seg = nx // ny
    lane = lane_of((nz, nx))
    part = lane % seg
    is_first = place_ref[0] == 1
    is_last = place_ref[1] == 1

    for k in range(fields):
        e = edge_ref[k]
        last = jnp.where(
            part == 10, pltpu.roll(e, 1, 1), jnp.where(part == 11, pltpu.roll(e, 2, 1), pltpu.roll(e, 3, 1))
        )
        lower = jnp.where(is_first, in_ref[k], left_ref[k])
        upper = jnp.where(is_last, last, right_ref[k])
        e = jnp.where(part < 3, lower, jnp.where((part >= 10) & (part < 13), upper, e))
        c = pltpu.roll(e, nx - 1, 1) - e
        ring[k] = c
        up, down = cell_faces(
            k, pltpu.roll(c, 2, 1), pltpu.roll(c, 1, 1), c, pltpu.roll(c, nx - 1, 1), e
        )
        sides[k] = up
        sides[fields + k] = down

    def stream(y, _):
        base = y * seg
        left, right = [], []
        at_seam = lane == base + 10
        for k in range(fields):
            h = w_ref[y, k]
            de = ring[k]
            tail = pltpu.roll(de, nx - 11 - base, 1)
            head = pltpu.roll(de, nx - 1 - base, 1)
            c = jnp.where(lane == nx - 1, pltpu.roll(tail, 1, 1), pltpu.roll(h, nx - 1, 1) - h)
            d = jnp.where(lane == nx - 1, tail, pltpu.roll(c, nx - 1, 1))
            a = jnp.where(lane < 2, head, pltpu.roll(c, 2, 1))
            b = jnp.where(lane < 1, pltpu.roll(head, nx - 1, 1), pltpu.roll(c, 1, 1))
            up, down = cell_faces(k, a, b, c, d, h)
            seam[k] = jnp.where(at_seam, pltpu.roll(up, base + 11, 1), seam[k])
            edge_up = pltpu.roll(sides[k], nx - base - 2, 1)
            left.append(jnp.where(lane < 1, edge_up, pltpu.roll(up, 1, 1)))
            right.append(down)
        flux = face_flux(left, right, 0)
        for k in range(fields + 1):
            flux_ref[y, k] = flux[k]
        return 0

    lax.fori_loop(0, ny, stream, 0)
    outer = face_flux(
        [seam[k] for k in range(fields)], [sides[fields + k] for k in range(fields)], 0
    )
    for k in range(fields + 1):
        keep[k] = outer[k]

    for y in range(ny):
        diff = []
        for k in range(fields + 1):
            f = flux_ref[y, k]
            end = pltpu.roll(keep[k], (2 * nx - 1 - 10 - y * seg) % nx, 1)
            diff.append(jnp.where(lane == nx - 1, end, pltpu.roll(f, nx - 1, 1)) - f)
        for k in range(fields):
            rate = acc_ref[y, k] - diff[k]
            if k == 6:
                rate = rate + w_ref[y, 6] * diff[7]
            rate_ref[y, k] = rate


def update_kernel(rate_ref, mine_ref, peer_ref, now_ref, base_ref, out_ref):
    ny, _, nz, nx = rate_ref.shape
    fastest = jnp.max(jnp.maximum(mine_ref[...], peer_ref[...]))
    step = (2.0 / 3.0) * (courant / jnp.full((nz, nx), fastest, jnp.float32))
    for y in range(ny):
        for k in range(fields):
            old = base_ref[k, :, y, :] * (1.0 / 3.0) + (2.0 / 3.0) * now_ref[k, :, y, :]
            out_ref[k, :, y, :] = old + step * rate_ref[y, k]


def buffer(*shape):
    return pltpu.VMEM(shape, jnp.float32)


def near(*arrays):
    return [pltpu.with_memory_space_constraint(x, pltpu.VMEM) for x in arrays]


def ring_pairs(size, shift):
    return [(i, (i + shift) % size) for i in range(size)]


def hop_pairs(size, hop, shift):
    if size & (size - 1) == 0 and size > 1:
        return [(i, i ^ hop) for i in range(size)]
    return ring_pairs(size, shift)


def shards(state_now, state_base, inflow):
    _, nz, ny, nx = state_now.shape
    width = ghost * fields + 1
    wide = buffer(ny, fields, nz, nx)
    vmem = pl.BlockSpec(memory_space=pltpu.VMEM)
    state_now, state_base = near(state_now, state_base)
    w, up, down, edge = pl.pallas_call(
        pack_kernel,
        out_shape=(wide, buffer(width, nz, nx), buffer(width, nz, nx), buffer(fields + 1, nz, nx)),
        in_specs=[vmem] * 2,
        out_specs=(vmem,) * 4,
        name="pack",
    )(state_now, state_base)

    streams, crosses = lax.axis_size("stream"), lax.axis_size("cross")
    low = lax.ppermute(up, "cross", ring_pairs(crosses, 1))
    high = lax.ppermute(down, "cross", ring_pairs(crosses, -1))
    left = lax.ppermute(edge, "stream", ring_pairs(streams, 1))
    right = lax.ppermute(edge, "stream", ring_pairs(streams, -1))

    rate, inner = pl.pallas_call(
        span_kernel,
        out_shape=(wide, buffer(fields, nz, nx)),
        in_specs=[vmem] * 2,
        out_specs=(vmem,) * 2,
        name="span",
    )(*near(w, jnp.transpose(inflow, (0, 3, 1, 2))))

    position = lax.axis_index("stream")
    place = jnp.stack([position == 0, position == streams - 1]).astype(jnp.int32)

    def cross_sweep():
        return pl.pallas_call(
            cross_kernel,
            out_shape=wide,
            in_specs=[vmem] * 4,
            out_specs=vmem,
            scratch_shapes=[
                buffer(ny + 2 * ghost, fields, nz, nx),
                buffer(2 * fields + 1, nz, nx),
            ],
            name="cross",
        )(*near(w, rate, low, high))

    def stream_sweep(acc):
        return pl.pallas_call(
            stream_kernel,
            out_shape=wide,
            in_specs=[pl.BlockSpec(memory_space=pltpu.SMEM)] + [vmem] * 6,
            out_specs=vmem,
            scratch_shapes=[
                buffer(fields, nz, nx),
                buffer(2 * fields, nz, nx),
                buffer(fields, nz, nx),
                buffer(ny, fields + 1, nz, nx),
                buffer(fields + 1, nz, nx),
            ],
            name="stream",
        )(place, *near(w, edge, left, right, inner, acc))

    speed = jnp.maximum(jnp.maximum(low[-1], high[-1]), edge[-1])
    speed, rate = lax.optimization_barrier((speed, rate))
    reach = 3
    while reach < crosses:
        ahead = lax.ppermute(speed, "cross", ring_pairs(crosses, reach))
        behind = lax.ppermute(speed, "cross", ring_pairs(crosses, -reach))
        speed = jnp.maximum(speed, jnp.maximum(ahead, behind))
        reach *= 3
    acc = cross_sweep()
    hop = 1
    while 2 * hop < streams:
        pairs = hop_pairs(streams, hop, hop)
        speed = jnp.maximum(speed, lax.ppermute(speed, "stream", pairs))
        hop *= 2
    speed, acc = lax.optimization_barrier((speed, acc))
    peer = lax.ppermute(speed, "stream", hop_pairs(streams, hop, streams - hop))
    rate = stream_sweep(acc)
    return pl.pallas_call(
        update_kernel,
        out_shape=jax.ShapeDtypeStruct(state_now.shape, jnp.float32),
        in_specs=[vmem] * 5,
        out_specs=vmem,
        name="update",
    )(*near(rate, speed, peer, state_now, state_base))


def solution(mesh):
    return jax.shard_map(
        shards,
        mesh=mesh,
        in_specs=(
            P(None, None, "cross", "stream"),
            P(None, None, "cross", "stream"),
            P(None, None, "cross", None),
        ),
        out_specs=P(None, None, "cross", "stream"),
        check_vma=False,
    )
```

```python
import jax
import jax.numpy as jnp
from jax import lax
from jax.experimental import pallas as pl
from jax.experimental.pallas import tpu as pltpu
from jax.sharding import PartitionSpec as P

gas_gamma = 1.4
liquid_gamma = 4.4
liquid_stiff = 0.6
courant = 0.3
weno_epsilon = 1e-06
ghost = 3
fields = 7


def reciprocal(value):
    guess = pl.reciprocal(value, approx=True)
    return guess * (2.0 - value * guess)


def mixture(volume):
    rest = 1.0 - volume
    stiff_gamma = volume * (1.0 / (gas_gamma - 1.0)) + rest * (1.0 / (liquid_gamma - 1.0))
    stiff_term = rest * (liquid_gamma * liquid_stiff / (liquid_gamma - 1.0))
    return stiff_gamma, stiff_term


def primitive(u):
    inverse = reciprocal(u[0] + u[1])
    v = [u[2] * inverse, u[3] * inverse, u[4] * inverse]
    kinetic = 0.5 * (u[2] * v[0] + u[3] * v[1] + u[4] * v[2])
    stiff_gamma, stiff_term = mixture(u[6])
    pressure = (u[5] - kinetic - stiff_term) * reciprocal(stiff_gamma)
    return [u[0], u[1], v[0], v[1], v[2], pressure, u[6]]


def sound(w, density, stiff_gamma, stiff_term):
    top = (stiff_gamma + 1.0) * w[5] + stiff_term
    return jnp.sqrt(top * reciprocal(stiff_gamma * density))


def weno_cell(a, b, c, d, h):
    low, mid, high = b - a, c - b, d - c
    e_low, e_mid, e_high = 3.0 * b - a, b + c, d - 3.0 * c

    def weight(bend, slope):
        smooth = weno_epsilon + (13.0 / 12.0) * (bend * bend) + 0.25 * (slope * slope)
        r = reciprocal(jnp.minimum(smooth, 1e38))
        return r * r

    w_low, w_mid, w_high = weight(low, e_low), 6.0 * weight(mid, e_mid), weight(high, e_high)
    low3, high3 = 3.0 * w_low, 3.0 * w_high
    total_up = (w_low + high3) + w_mid
    total_down = (low3 + w_high) + w_mid
    up = w_low * (5.0 * b - 2.0 * a) + w_mid * (b + 2.0 * c) + high3 * (4.0 * c - d)
    down = w_high * (5.0 * c - 2.0 * d) + w_mid * (c + 2.0 * b) + low3 * (4.0 * b - a)
    up = h + up * (reciprocal(total_up) * (1.0 / 6.0))
    down = h - down * (reciprocal(total_down) * (1.0 / 6.0))
    return up, down


def limit(component, value, first, second):
    if component in (0, 1, 5):
        return jnp.maximum(value, 0.5 * jnp.minimum(first, second))
    if component == 6:
        smaller = 0.5 * jnp.minimum(first, second)
        larger = 1.0 - 0.5 * (1.0 - jnp.maximum(first, second))
        return jnp.minimum(jnp.maximum(value, smaller), larger)
    return value


def cell_faces(component, a, b, c, d, h):
    up, down = weno_cell(a, b, c, d, h)
    return limit(component, up, h, h + c), limit(component, down, h - b, h)


def side_terms(w, normal):
    density = w[0] + w[1]
    stiff_gamma, stiff_term = mixture(w[6])
    v = w[2:5]
    mom = [density * x for x in v]
    energy = stiff_gamma * w[5] + stiff_term + 0.5 * (mom[0] * v[0] + mom[1] * v[1] + mom[2] * v[2])
    vn = v[normal]
    amounts = [w[0], w[1], mom[0], mom[1], mom[2], energy, w[6]]
    moved = [x * vn for x in amounts]
    moved[2 + normal] = moved[2 + normal] + w[5]
    moved[5] = moved[5] + w[5] * vn
    return amounts, moved, vn, jnp.abs(vn) + sound(w, density, stiff_gamma, stiff_term)


def face_flux(left, right, normal):
    ul, fl, vl, sl = side_terms(left, normal)
    ur, fr, vr, sr = side_terms(right, normal)
    half = 0.5 * jnp.maximum(sl, sr)
    flux = [0.5 * (fl[i] + fr[i]) - half * (ur[i] - ul[i]) for i in range(fields)]
    return flux + [0.5 * (vl + vr)]


def lane_of(shape):
    return lax.broadcasted_iota(jnp.int32, shape, 1)


def pack_kernel(
    now_hbm, base_hbm, w_ref, up_ref, down_ref, edge_ref, old_ref, now_ref, base_ref, sems
):
    nz, ny, nx = now_ref.shape[1:]
    seg = nx // ny
    lane = lane_of((nz, nx))

    loads = []
    for i, (src, dst) in enumerate(((now_hbm, now_ref), (base_hbm, base_ref))):
        for c in range(fields):
            loads.append(pltpu.make_async_copy(src.at[c], dst.at[c], sems.at[i * fields + c]))
    for load in loads:
        load.start()
    for load in loads[:fields]:
        load.wait()
    for y in range(ny):
        w = primitive([now_ref[c, :, y, :] for c in range(fields)])
        first = (lane >= y * seg) & (lane < y * seg + 6)
        mine = (lane >= y * seg) & (lane < (y + 1) * seg)
        for c in range(fields):
            w_ref[y, c] = w[c]
            if y >= ny - ghost:
                up_ref[(y - ny + ghost) * fields + c] = w[c]
            if y < ghost:
                down_ref[y * fields + c] = w[c]
            low = pltpu.roll(w[c], (y * seg + 3) % nx, 1)
            high = pltpu.roll(w[c], (y * seg + 10) % nx, 1)
            both = jnp.where(first, low, high)
            edge_ref[c] = both if y == 0 else jnp.where(mine, both, edge_ref[c])
    for load in loads[fields:]:
        load.wait()
    fastest = None
    for y in range(ny):
        b = [base_ref[c, :, y, :] for c in range(fields)]
        for c in range(fields):
            old_ref[y, c] = b[c] * (1.0 / 3.0) + (2.0 / 3.0) * now_ref[c, :, y, :]
        b = primitive(b)
        stiff_gamma, stiff_term = mixture(b[6])
        speed = jnp.maximum(jnp.maximum(jnp.abs(b[2]), jnp.abs(b[3])), jnp.abs(b[4]))
        speed = speed + sound(b, b[0] + b[1], stiff_gamma, stiff_term)
        fastest = speed if fastest is None else jnp.maximum(fastest, speed)
    up_ref[ghost * fields] = fastest
    down_ref[ghost * fields] = fastest
    edge_ref[fields] = fastest


def span_kernel(w_ref, inflow_ref, rate_ref, in_ref):
    ny, _, nz, nx = w_ref.shape
    seg = nx // ny

    def plane(y, _):
        left, right = [], []
        for k in range(fields):
            h = w_ref[y, k]
            c = pltpu.roll(h, nz - 1, 0) - h
            b = pltpu.roll(c, 1, 0)
            a = pltpu.roll(c, 2, 0)
            d = pltpu.roll(c, nz - 1, 0)
            up, down = cell_faces(k, a, b, c, d, h)
            left.append(pltpu.roll(up, 1, 0))
            right.append(down)
        flux = face_flux(left, right, 2)
        diff = [pltpu.roll(f, nz - 1, 0) - f for f in flux]
        for k in range(fields):
            rate_ref[y, k] = -diff[k] if k < 6 else w_ref[y, 6] * diff[7] - diff[6]
        return 0

    lax.fori_loop(0, ny, plane, 0)

    lane = lane_of((nz, nx))
    layers = []
    for c in range(fields):
        packed = jnp.ones((nz, nx), jnp.float32)
        for g in range(ghost):
            layer = jnp.concatenate(
                [inflow_ref[c, g], jnp.zeros((nz, nx - ny), jnp.float32)], axis=1
            )
            for y in range(ny):
                shift = (y * seg + g - y) % nx
                moved = layer if shift == 0 else pltpu.roll(layer, shift, 1)
                packed = jnp.where(lane == y * seg + g, moved, packed)
        layers.append(packed)
    layers = primitive(layers)
    for c in range(fields):
        in_ref[c] = layers[c]


def cross_kernel(w_ref, rate_ref, low_ref, high_ref, acc, tall, keep):
    ny = w_ref.shape[0]

    for y in range(ghost):
        for c in range(fields):
            tall[y, c] = low_ref[y * fields + c]
            tall[ghost + ny + y, c] = high_ref[y * fields + c]

    def copy(y, _):
        tall[y + ghost] = w_ref[y]
        return 0

    lax.fori_loop(0, ny, copy, 0)

    def cross(i, _):
        left = [keep[k] for k in range(fields)]
        right = []
        for k in range(fields):
            f, g, h, kk, l = [tall[i + o, k] for o in range(5)]
            up, down = cell_faces(k, g - f, h - g, kk - h, l - kk, h)
            keep[k] = up
            right.append(down)

        @pl.when(i > 0)
        def _():
            flux = face_flux(left, right, 1)

            @pl.when(i > 1)
            def _():
                y = i - 2
                diff = [flux[k] - keep[fields + k] for k in range(fields + 1)]
                for k in range(6):
                    acc[y, k] = rate_ref[y, k] - diff[k]
                acc[y, 6] = rate_ref[y, 6] - diff[6] + w_ref[y, 6] * diff[7]

            for k in range(fields + 1):
                keep[fields + k] = flux[k]

        return 0

    lax.fori_loop(0, ny + 2, cross, 0)


def stream_kernel(
    w_ref, edge_ref, left_ref, right_ref, in_ref, acc_ref, rate_ref, ring, flux_ref, keep
):
    ny, _, nz, nx = w_ref.shape
    seg = nx // ny
    lane = lane_of((nz, nx))
    part = lane % seg
    is_first = left_ref[fields] <= 0.0
    is_last = right_ref[fields] <= 0.0

    left, right = [], []
    for k in range(fields):
        e = edge_ref[k]
        last = jnp.where(
            part == 10, pltpu.roll(e, 1, 1), jnp.where(part == 11, pltpu.roll(e, 2, 1), pltpu.roll(e, 3, 1))
        )
        lower = jnp.where(is_first, in_ref[k], left_ref[k])
        upper = jnp.where(is_last, last, right_ref[k])
        e = jnp.where(part < 3, lower, jnp.where((part >= 10) & (part < 13), upper, e))
        ring[k] = jnp.where(part < 3, e, pltpu.roll(e, nx - 7, 1))
        c = pltpu.roll(e, nx - 1, 1) - e
        up, down = cell_faces(
            k, pltpu.roll(c, 2, 1), pltpu.roll(c, 1, 1), c, pltpu.roll(c, nx - 1, 1), e
        )
        left.append(pltpu.roll(up, 1, 1))
        right.append(down)
    outer = face_flux(left, right, 0)
    for k in range(fields + 1):
        keep[k] = jnp.where(part == 2, pltpu.roll(outer[k], nx - 8, 1), outer[k])

    def stream(y, _):
        base = y * seg
        left, right = [], []
        for k in range(fields):
            h = w_ref[y, k]
            beyond = pltpu.roll(ring[k], nx - 3 - base, 1)
            f = pltpu.roll(jnp.where(lane >= nx - 2, beyond, h), 2, 1)
            g = pltpu.roll(jnp.where(lane == nx - 1, beyond, h), 1, 1)
            kk = pltpu.roll(jnp.where(lane == 0, beyond, h), nx - 1, 1)
            l = pltpu.roll(jnp.where(lane < 2, beyond, h), nx - 2, 1)
            up, down = cell_faces(k, g - f, h - g, kk - h, l - kk, h)
            left.append(pltpu.roll(up, 1, 1))
            right.append(down)
        flux = face_flux(left, right, 0)
        for k in range(fields + 1):
            flux_ref[y, k] = flux[k]
        return 0

    lax.fori_loop(0, ny, stream, 0)
    for y in range(ny):
        diff = []
        for k in range(fields + 1):
            f = flux_ref[y, k]
            ends = pltpu.roll(keep[k], (nx - 3 - y * seg) % nx, 1)
            here = jnp.where(lane == 0, ends, f)
            after = jnp.where(lane == nx - 1, ends, pltpu.roll(f, nx - 1, 1))
            diff.append(after - here)
        for k in range(fields):
            rate = acc_ref[y, k] - diff[k]
            if k == 6:
                rate = rate + w_ref[y, 6] * diff[7]
            rate_ref[y, k] = rate


def update_kernel(rate_ref, mine_ref, peer_ref, old_ref, out_hbm, out_ref, sems):
    ny, _, nz, nx = rate_ref.shape
    fastest = jnp.max(jnp.maximum(mine_ref[...], peer_ref[...]))
    step = (2.0 / 3.0) * (courant / jnp.full((nz, nx), fastest, jnp.float32))
    stores = []
    for k in range(fields):
        for y in range(ny):
            out_ref[k, :, y, :] = old_ref[y, k] + step * rate_ref[y, k]
        stores.append(pltpu.make_async_copy(out_ref.at[k], out_hbm.at[k], sems.at[k]))
        stores[-1].start()
    for store in stores:
        store.wait()


def buffer(*shape):
    return pltpu.VMEM(shape, jnp.float32)


def near(*arrays):
    return [pltpu.with_memory_space_constraint(x, pltpu.VMEM) for x in arrays]


def ring_pairs(size, shift):
    return [(i, (i + shift) % size) for i in range(size)]


def hop_pairs(size, hop, shift):
    if size & (size - 1) == 0 and size > 1:
        return [(i, i ^ hop) for i in range(size)]
    return ring_pairs(size, shift)


def shards(state_now, state_base, inflow):
    _, nz, ny, nx = state_now.shape
    width = ghost * fields + 1
    wide = buffer(ny, fields, nz, nx)
    vmem = pl.BlockSpec(memory_space=pltpu.VMEM)
    whole = pl.BlockSpec(memory_space=pl.ANY)
    w, up, down, edge, old = pl.pallas_call(
        pack_kernel,
        out_shape=(
            wide,
            buffer(width, nz, nx),
            buffer(width, nz, nx),
            buffer(fields + 1, nz, nx),
            wide,
        ),
        in_specs=[whole] * 2,
        out_specs=(vmem,) * 5,
        scratch_shapes=[
            buffer(fields, nz, ny, nx),
            buffer(fields, nz, ny, nx),
            pltpu.SemaphoreType.DMA((2 * fields,)),
        ],
        name="pack",
    )(state_now, state_base)

    streams, crosses = lax.axis_size("stream"), lax.axis_size("cross")
    low = lax.ppermute(up, "cross", ring_pairs(crosses, 1))
    high = lax.ppermute(down, "cross", ring_pairs(crosses, -1))
    onward = [(i, i + 1) for i in range(streams - 1)]
    left = lax.ppermute(edge, "stream", onward)
    right = lax.ppermute(edge, "stream", [(j, i) for i, j in onward])

    rate, inner = pl.pallas_call(
        span_kernel,
        out_shape=(wide, buffer(fields, nz, nx)),
        in_specs=[vmem] * 2,
        out_specs=(vmem,) * 2,
        name="span",
    )(*near(w, jnp.transpose(inflow, (0, 3, 1, 2))))

    def cross_sweep():
        return pl.pallas_call(
            cross_kernel,
            out_shape=wide,
            in_specs=[vmem] * 4,
            out_specs=vmem,
            scratch_shapes=[
                buffer(ny + 2 * ghost, fields, nz, nx),
                buffer(2 * fields + 1, nz, nx),
            ],
            name="cross",
        )(*near(w, rate, low, high))

    def stream_sweep(acc):
        return pl.pallas_call(
            stream_kernel,
            out_shape=wide,
            in_specs=[vmem] * 6,
            out_specs=vmem,
            scratch_shapes=[
                buffer(fields, nz, nx),
                buffer(ny, fields + 1, nz, nx),
                buffer(fields + 1, nz, nx),
            ],
            name="stream",
        )(*near(w, edge, left, right, inner, acc))

    speed = jnp.maximum(jnp.maximum(low[-1], high[-1]), edge[-1])
    speed, rate = lax.optimization_barrier((speed, rate))
    reach = 3
    while reach < crosses:
        ahead = lax.ppermute(speed, "cross", ring_pairs(crosses, reach))
        behind = lax.ppermute(speed, "cross", ring_pairs(crosses, -reach))
        speed = jnp.maximum(speed, jnp.maximum(ahead, behind))
        reach *= 3
    acc = cross_sweep()
    hop = 1
    while 2 * hop < streams:
        pairs = hop_pairs(streams, hop, hop)
        speed = jnp.maximum(speed, lax.ppermute(speed, "stream", pairs))
        hop *= 2
    speed, acc = lax.optimization_barrier((speed, acc))
    peer = lax.ppermute(speed, "stream", hop_pairs(streams, hop, streams - hop))
    rate = stream_sweep(acc)
    return pl.pallas_call(
        update_kernel,
        out_shape=jax.ShapeDtypeStruct(state_now.shape, jnp.float32),
        in_specs=[vmem] * 4,
        out_specs=whole,
        scratch_shapes=[
            buffer(fields, nz, ny, nx),
            pltpu.SemaphoreType.DMA((fields,)),
        ],
        name="update",
    )(*near(rate, speed, peer, old))


def solution(mesh):
    return jax.shard_map(
        shards,
        mesh=mesh,
        in_specs=(
            P(None, None, "cross", "stream"),
            P(None, None, "cross", "stream"),
            P(None, None, "cross", None),
        ),
        out_specs=P(None, None, "cross", "stream"),
        check_vma=False,
    )
```
